512 devices in a mesh: seq: 64 (over x, z_lo, core), tp: 8 (over z_hi, y).
Axes of the slice: x: 4, y: 4, z: 16 (z_hi: 2, z_lo: 8; z = z_hi * 8 + z_lo), core: 2. Of those that a mesh axis runs over, the one named last changes fastest.
Arguments:
- stream_x: bfloat16 [8192, 4096], P('seq', 'tp'), may hold values from -6 to 6
- norm_gain: float32 [4096], replicated, may hold values from 0.1 to 1.9
- w_qkv: bfloat16 [4096, 6144], P('seq', 'tp'), may hold values from -0.09375 to 0.09375
- cache_kv: bfloat16 [2, 4096, 1024], P(None, 'seq', 'tp'), may hold values from -400 to 400
- recomp_hidden: bfloat16 [512, 4096], P('seq', 'tp'), may hold values from -6 to 6
- recomp_index: int32 [512], P('seq'), may hold values from 0 to 4095, as said below
- prefix_len: int32 [1], replicated, may hold values from 2048 to 4096
Outputs:
- attended: bfloat16 [8192, 4096], P('seq', 'tp')
The draws below stay inside these ranges and needn't reach their ends.
Inputs may be any that keep to these rules, and one draw needn't show every extreme that they name: `recomp_index`: the entries held by index s of seq name distinct cache rows of s * 64 to s * 64 + 63.
All inputs are finite; a program needn't handle non-finite values.
Results may differ from the reference program's by a relative error of at most 0.015.
The reference program's roundings to bfloat16 on the way count: a program that leaves them out, or rounds other values in their place, can miss the bound.
Values may be sent and summed in bfloat16 or wider, within the bound.
A program may use at most 64 MiB of HBM per device.

```python
import math
import jax
import jax.numpy as jnp
from jax import lax

D = 4096
HEADS = 32
KVH = 8
HD = 128
GROUP = 4
CACHE_DEV = 64
RECOMP_DEV = 8
STREAM = 8192
CACHE = 4096
RECOMP = 512


def draw_recomp_index(key, part):
    blocks = CACHE // CACHE_DEV
    subkeys = jax.random.split(jax.random.fold_in(key, 11), blocks)
    offsets = jax.vmap(lambda k: jax.random.permutation(k, CACHE_DEV)[:RECOMP_DEV])(subkeys)
    base = jnp.arange(blocks, dtype=jnp.int32)[:, None] * CACHE_DEV
    return (offsets.astype(jnp.int32) + base).reshape(-1).astype(jnp.int32)


def draw_cache_kv(key, part):
    base = jax.random.normal(jax.random.fold_in(key, 21), (2, CACHE, KVH * HD), jnp.float32)
    base = jnp.clip(base, -6.0, 6.0)
    return base.astype(jnp.bfloat16)


def shard_levels(own_key, extent, cuts, least, largest):
    factor_of = 1.0
    for dim, parts in cuts:
        steps = jax.random.uniform(jax.random.fold_in(jax.random.fold_in(own_key, 6), dim), (parts,), jnp.float32, least / len(cuts), largest / len(cuts))
        factor_of = factor_of * jnp.repeat(jnp.exp(steps), extent[dim] // parts).reshape((-1,) + (1,) * (len(extent) - 1 - dim))
    return factor_of


def gaussian(key, shape, scale, most, shards=(), kind=jnp.bfloat16):
    level = shard_levels(key, shape, shards, -0.22, 0.18) if shards else 1.0
    values = jax.random.normal(key, shape, jnp.float32) * scale * level
    return jnp.minimum(jnp.maximum(values, -most), most).astype(kind)


def setup_inputs(seed: int = 0) -> dict:
    seeds = jax.random.split(jax.random.key(seed), 8)
    return {
        "stream_x": gaussian(seeds[0], (STREAM, D), 1.0, 6.0, ((0, 64), (1, 8))),
        "norm_gain": jnp.clip(1.0 + 0.18 * jax.random.normal(seeds[1], (D,), jnp.float32), 0.1, 1.9),
        "w_qkv": gaussian(seeds[2], (D, (GROUP + 2) * HD * KVH), D ** -0.5, 0.09375, ((0, 64), (1, 8))),
        "cache_kv": draw_cache_kv(jax.random.fold_in(seeds[7], 71), 0),
        "recomp_hidden": gaussian(seeds[4], (RECOMP, D), 1.0, 6.0, ((0, 64), (1, 8))),
        "recomp_index": draw_recomp_index(jax.random.fold_in(seeds[7], 71), 0),
        "prefix_len": jax.random.randint(seeds[6], (1,), CACHE // 2, CACHE + 1).astype(jnp.int32),
    }


def normed(rows, gain):
    values = rows.astype(jnp.float32)
    spread = lax.optimization_barrier(jnp.mean(values * values, axis=-1, keepdims=True))
    return (values * lax.rsqrt(spread + 1e-05) * gain.astype(jnp.float32)).astype(jnp.bfloat16)

def rotate(values, places):
    half = values.shape[-1] // 2
    freq = jnp.exp(-math.log(1000000.0) * jnp.arange(half, dtype=jnp.float32) * 2.0 / (2 * half))
    angle = places[:, None] * freq[None, :]
    shape = (angle.shape[0],) + (1,) * (values.ndim - 2) + (half,)
    cosine = jnp.cos(angle).reshape(shape)
    sine = jnp.sin(angle).reshape(shape)
    first = values[..., :half]
    second = values[..., half:]
    return jnp.concatenate([first * cosine - second * sine, first * sine + second * cosine], -1)

def reference(stream_x, norm_gain, w_qkv, cache_kv, recomp_hidden, recomp_index, prefix_len):
    group = HEADS // KVH
    normed_x = normed(stream_x, norm_gain)
    normed_h = normed(recomp_hidden, norm_gain)
    proj = jnp.dot(normed_x, w_qkv, preferred_element_type=jnp.float32).reshape(STREAM, KVH, group + 2, HD)
    proj_h = jnp.dot(normed_h, w_qkv, preferred_element_type=jnp.float32).reshape(RECOMP, KVH, group + 2, HD)
    begin = prefix_len[0]
    token_ids = jnp.arange(STREAM, dtype=jnp.int32)
    places = (token_ids + begin).astype(jnp.float32)
    query = rotate(proj[:, :, :group], places).astype(jnp.bfloat16)
    new_keys = rotate(proj[:, :, group], places).astype(jnp.bfloat16)
    new_values = proj[:, :, group + 1].astype(jnp.bfloat16)
    redo_keys = rotate(proj_h[:, :, group], recomp_index.astype(jnp.float32)).astype(jnp.bfloat16)
    redo_values = proj_h[:, :, group + 1].astype(jnp.bfloat16)
    keys_c = cache_kv[0].reshape(CACHE, KVH, HD).at[recomp_index].set(redo_keys)
    values_c = cache_kv[1].reshape(CACHE, KVH, HD).at[recomp_index].set(redo_values)
    all_keys = jnp.transpose(jnp.concatenate([keys_c, new_keys], 0), (1, 0, 2))
    all_values = jnp.transpose(jnp.concatenate([values_c, new_values], 0), (1, 0, 2))
    query_heads = jnp.transpose(query, (1, 0, 2, 3))
    cache_ok = jnp.arange(CACHE, dtype=jnp.int32) < begin
    scale = 1.0 / math.sqrt(HD)
    block = math.gcd(STREAM, 512)

    def one_head(items):
        q_all, key_rows, value_rows = items
        key_f = key_rows.astype(jnp.float32)
        value_f = value_rows.astype(jnp.float32)

        def one_block(index):
            first = index * block
            q_blk = lax.dynamic_slice_in_dim(q_all, first, block, 0).astype(jnp.float32)
            score = jnp.einsum('qhd,nd->hqn', q_blk, key_f) * scale
            rows = first + jnp.arange(block, dtype=jnp.int32)
            stream_ok = token_ids[None, :] <= rows[:, None]
            allowed = jnp.concatenate([jnp.broadcast_to(cache_ok[None, :], (block, CACHE)), stream_ok], 1)
            score = jnp.where(allowed[None], score, -1e+30)
            top = lax.optimization_barrier(jnp.max(score, -1, keepdims=True))
            weights = jnp.where(allowed[None], jnp.exp(score - top), 0.0)
            total = lax.optimization_barrier(jnp.sum(weights, -1))
            mixed = jnp.einsum('hqn,nd->hqd', weights.astype(jnp.bfloat16).astype(jnp.float32), value_f)
            mixed = mixed / total[..., None]
            return jnp.transpose(mixed, (1, 0, 2))
        outs = lax.map(one_block, jnp.arange(STREAM // block, dtype=jnp.int32))
        return outs.reshape(STREAM, group, HD)
    result = lax.map(one_head, (query_heads, all_keys, all_values))
    return jnp.transpose(result, (1, 0, 2, 3)).reshape(STREAM, HEADS * HD).astype(jnp.bfloat16)
```

```python
import functools
import math

import jax
import jax.numpy as jnp
from jax import lax
from jax.experimental import pallas as pl
from jax.experimental.pallas import tpu as pltpu
from jax.sharding import PartitionSpec as P

HEADS = 32
KVH = 8
HD = 128
GROUP = HEADS // KVH
NX, NZ, NC = 4, 8, 2
NY, NH = 4, 2
MESH = pl.DeviceIdType.MESH
F32 = jnp.float32
BF16 = jnp.bfloat16
LOW = -1e30
SCALE = 1.0 / math.sqrt(HD)


class Gather:
    def __init__(self, buf, recv, side, zsend, xsend, csend):
        self.buf, self.recv, self.side = buf, recv, side
        self.zsend, self.xsend, self.csend = zsend, xsend, csend
        s = lax.axis_index("seq")
        self.x, self.z, self.c = s // (NZ * NC), (s // NC) % NZ, s % NC

    def dev(self, x, z, c):
        return ((x + NX) % NX) * (NZ * NC) + z * NC + c

    def column(self, o):
        return (self.x + o // 2 + (o % 2) * (3 - 2 * (o // 2))) % NX

    def ok(self, t, g):
        j = self.z + (2 * g - 1) * t
        return (t >= 0) & (t + g >= 0) & (t < NZ) & (j >= 0) & (j < NZ) & ((t > 0) | (g == 0))

    def copy(self, block, send, recv, target):
        return pltpu.make_async_remote_copy(
            src_ref=self.buf.at[block],
            dst_ref=self.buf.at[block],
            send_sem=send,
            recv_sem=recv,
            device_id={"seq": target},
            device_id_type=MESH,
        )

    def to_side(self, block, o, t, g):
        self.copy(block, self.csend, self.side.at[o, t, g], self.dev(self.x, self.z, 1 - self.c)).start()

    def wait(self, sems, block, o, t, g):
        self.copy(block, self.csend, sems.at[o, t, g], self.dev(self.x, self.z, 1 - self.c)).wait_recv()

    def first(self):
        block = self.dev(self.x, self.z, self.c)

        @pl.when(self.z < NZ - 1)
        def _():
            self.copy(block, self.zsend, self.recv.at[0, 1, 0], self.dev(self.x, self.z + 1, self.c)).start()

        @pl.when(self.z > 0)
        def _():
            self.copy(block, self.zsend, self.recv.at[0, 1, 1], self.dev(self.x, self.z - 1, self.c)).start()

        self.spread(block, 0, 0)

    def spread(self, block, t, g):
        self.copy(block, self.xsend, self.recv.at[1, t, g], self.dev(self.x + 1, self.z, self.c)).start()
        self.copy(block, self.xsend, self.recv.at[2, t, g], self.dev(self.x - 1, self.z, self.c)).start()
        self.to_side(block, 0, t, g)

    def stage_a(self, t, g):
        d = 2 * g - 1

        @pl.when(self.ok(t, g) & (t > 0))
        def _():
            block = self.dev(self.x, self.z + d * t, self.c)
            self.wait(self.recv, block, 0, t, g)
            after = self.z - d

            @pl.when((after >= 0) & (after < NZ))
            def _():
                self.copy(block, self.zsend, self.recv.at[0, t + 1, g], self.dev(self.x, after, self.c)).start()

            self.spread(block, t, g)

    def stage_b(self, t, g):
        d = 2 * g - 1

        @pl.when(self.ok(t, g))
        def _():
            even = (t + g) % 2 == 0
            left = self.dev(self.x - 1, self.z + d * t, self.c)
            self.wait(self.recv, left, 1, t, g)

            @pl.when(even)
            def _():
                self.copy(left, self.xsend, self.recv.at[3, t, g], self.dev(self.x + 1, self.z, self.c)).start()

            self.to_side(left, 1, t, g)
            right = self.dev(self.x + 1, self.z + d * t, self.c)
            self.wait(self.recv, right, 2, t, g)

            @pl.when(jnp.logical_not(even))
            def _():
                self.copy(right, self.xsend, self.recv.at[3, t, g], self.dev(self.x - 1, self.z, self.c)).start()

            self.to_side(right, 2, t, g)

    def stage_c(self, t, g):
        d = 2 * g - 1

        @pl.when(self.ok(t, g))
        def _():
            far = self.dev(self.x + 2, self.z + d * t, self.c)
            self.wait(self.recv, far, 3, t, g)
            self.to_side(far, 3, t, g)

    def wait_side(self, x, o, t, g):
        self.wait(self.side, self.dev(x, self.z + (2 * g - 1) * t, 1 - self.c), o, t, g)

    def finish_sends(self):
        def done(sem, count):
            pltpu.make_async_remote_copy(
                src_ref=self.buf.at[pl.ds(0, count)],
                dst_ref=self.buf.at[pl.ds(0, count)],
                send_sem=sem,
                recv_sem=self.recv.at[0, 0, 0],
                device_id={"seq": self.dev(self.x, self.z, 1 - self.c)},
                device_id_type=MESH,
            ).wait_send()

        done(self.xsend, 3 * NZ)
        done(self.csend, 4 * NZ)
        inner = (self.z > 0) & (self.z < NZ - 1)

        @pl.when(inner)
        def _():
            done(self.zsend, NZ + 1)

        @pl.when(jnp.logical_not(inner))
        def _():
            done(self.zsend, 1)


def kernel(
    prefix_ref, x_ref, h_ref, gain_ref, w_ref, cache_ref, index_ref, cos_ref, sin_ref,
    out_ref,
    xbuf, wbuf, kvbuf, nx, proj, qs, top, total, accum,
    xrecv, xsend, wrecv, wside, krecv, kside, sends,
):
    s = lax.axis_index("seq")
    tp = lax.axis_index("tp")
    c = s % NC
    y, h = tp % NY, tp // NY
    toks, redo = x_ref.shape[0], h_ref.shape[0]
    rows = xbuf.shape[1]
    cached = cache_ref.shape[1]
    gw = Gather(wbuf, wrecv, wside, sends.at[0], sends.at[1], sends.at[2])
    gk = Gather(kvbuf, krecv, kside, sends.at[3], sends.at[4], sends.at[5])
    x, z = gw.x, gw.z

    barrier = pltpu.get_barrier_semaphore()

    def hello(axis, target):
        pl.semaphore_signal(barrier, inc=1, device_id={axis: target}, device_id_type=MESH)

    y_right, y_left = h * NY + (y + 1) % NY, h * NY + (y + NY - 1) % NY
    over = (1 - h) * NY + y
    hello("seq", gw.dev(x + 1, z, c))
    hello("seq", gw.dev(x - 1, z, c))
    hello("seq", gw.dev(x, z, 1 - c))
    hello("tp", y_right)
    hello("tp", y_left)
    hello("tp", over)

    @pl.when(z > 0)
    def _():
        hello("seq", gw.dev(x, z - 1, c))

    @pl.when(z < NZ - 1)
    def _():
        hello("seq", gw.dev(x, z + 1, c))

    wbuf[s] = w_ref[...]
    xbuf[tp, pl.ds(0, toks)] = x_ref[...]
    xbuf[tp, pl.ds(toks, rows - toks)] = jnp.concatenate(
        [h_ref[...], jnp.zeros((rows - toks - redo, h_ref.shape[1]), BF16)], 0
    )

    @pl.when((z > 0) & (z < NZ - 1))
    def _():
        pl.semaphore_wait(barrier, 8)

    @pl.when((z == 0) | (z == NZ - 1))
    def _():
        pl.semaphore_wait(barrier, 7)

    def xcopy(piece, slot, target):
        return pltpu.make_async_remote_copy(
            src_ref=xbuf.at[piece],
            dst_ref=xbuf.at[piece],
            send_sem=xsend.at[slot],
            recv_sem=xrecv.at[slot],
            device_id={"tp": target},
            device_id_type=MESH,
        )

    other = (1 - h) * NY
    y2 = (y + 2) % NY
    xcopy(tp, 0, over).start()
    xcopy(tp, 1, y_right).start()
    xcopy(tp, 2, y_left).start()
    gw.first()

    def near_x():
        xcopy(y_left, 1, y_right).wait_recv()
        xcopy(y_left, 3, y_right).start()
        xcopy(y_right, 2, y_left).wait_recv()

    def over_x():
        xcopy(over, 0, over).wait_recv()
        xcopy(over, 4, y_right).start()
        xcopy(over, 5, y_left).start()

    def far_x():
        right = other + (y + 1) % NY
        xcopy(right, 5, y_left).wait_recv()
        xcopy(right, 6, y_left).start()
        xcopy(other + (y + NY - 1) % NY, 4, y_right).wait_recv()

    def last_x():
        xcopy(h * NY + y2, 3, y_right).wait_recv()
        xcopy(other + y2, 6, y_left).wait_recv()

    @pl.loop(0, NZ + 2)
    def _(t):
        for step, part in ((2, near_x), (4, over_x), (6, far_x)):
            pl.when(t == step)(part)

        @pl.loop(0, 2)
        def _(g):
            gw.stage_a(t, g)
            gw.stage_b(t - 1, g)
            gw.stage_c(t - 2, g)

    last_x()

    feats = xbuf.shape[2]
    square = jnp.zeros((rows, 1), F32)
    for piece in range(NY * NH):
        values = xbuf[piece].astype(F32)
        square = square + jnp.sum(values * values, axis=-1, keepdims=True)
    factor = lax.rsqrt(square * (1.0 / (feats * NY * NH)) + 1e-05)
    for piece in range(NY * NH):
        span = pl.ds(piece * feats, feats)
        values = xbuf[piece].astype(F32)
        nx[:, span] = (values * factor * gain_ref[:, span]).astype(BF16)

    @pl.loop(0, NZ)
    def _(t):
        @pl.loop(0, 2)
        def _(g):
            @pl.when(gw.ok(t, g))
            def _():
                gw.wait_side(x, 0, t, g)
                gw.wait_side(x - 1, 1, t, g)
                gw.wait_side(x + 1, 2, t, g)
                gw.wait_side(x + 2, 3, t, g)

    per = 8
    wrows = wbuf.shape[1]
    cols = wbuf.shape[2]
    proj[...] = jnp.zeros_like(proj)

    @pl.loop(0, (NX * NZ * NC) // per)
    def _(k):
        weights = wbuf[pl.ds(k * per, per)].reshape(per * wrows, cols)
        left = nx[:, pl.ds(pl.multiple_of(k * per * wrows, per * wrows), per * wrows)]
        proj[...] += jnp.dot(left, weights, preferred_element_type=F32)

    cosine, sine = cos_ref[...], sin_ref[...]

    def rotate(v, n):
        return v * cosine[:n] + pltpu.roll(v, HD // 2, 1) * sine[:n]

    for head in range(GROUP):
        qs[pl.ds(head * toks, toks)] = rotate(proj[pl.ds(0, toks), pl.ds(head * HD, HD)], toks).astype(BF16)
    keys = rotate(proj[:, pl.ds(GROUP * HD, HD)], rows).astype(BF16)
    values = proj[:, pl.ds((GROUP + 1) * HD, HD)].astype(BF16)
    extra = rows - toks
    hit = lax.broadcasted_iota(jnp.int32, (cached, extra), 0) == index_ref[...]
    pick = hit.astype(BF16)
    changed = jnp.sum(hit.astype(F32), axis=1, keepdims=True) > 0.0
    for kind, new in ((0, keys), (1, values)):
        base = kind * (toks + cached)
        kvbuf[s, pl.ds(base, toks)] = new[:toks]
        moved = jnp.dot(pick, new[toks:], preferred_element_type=F32).astype(BF16)
        kvbuf[s, pl.ds(base + toks, cached)] = jnp.where(changed, moved, cache_ref[kind])

    gk.first()

    begin = prefix_ref[0]
    half = toks + cached

    def attend(key, value, bias):
        n = key.shape[0]
        for head in range(GROUP):
            span = pl.ds(head * toks, toks)
            score = lax.dot_general(
                qs[span], key, (((1,), (1,)), ((), ())), preferred_element_type=F32
            ) * SCALE + bias
            top_old = top[span]
            top_new = jnp.maximum(top_old, jnp.max(score, axis=1, keepdims=True))
            keep = jnp.exp(top_old - top_new)
            weights = jnp.exp(score - top_new[:, :1])
            top[span] = top_new
            total[span] = total[span] * keep + jnp.sum(weights, axis=1, keepdims=True)
            accum[span] = accum[span] * keep + jnp.dot(
                weights.astype(BF16), value, preferred_element_type=F32
            )

    top[...] = jnp.full_like(top, LOW)
    total[...] = jnp.zeros_like(total)
    accum[...] = jnp.zeros_like(accum)

    def one_device(d, stream_ok):
        place = lax.broadcasted_iota(jnp.int32, (toks, half), 1)
        cache_ok = (d * cached + place - toks) < begin
        allowed = ((place < toks) & stream_ok(place)) | ((place >= toks) & cache_ok)
        attend(kvbuf[d, pl.ds(0, half)], kvbuf[d, pl.ds(half, half)], jnp.where(allowed, 0.0, LOW))

    one_device(s, lambda place: place <= lax.broadcasted_iota(jnp.int32, (toks, half), 0))

    def sibling():
        d = gk.dev(x, z, 1 - c)
        gk.wait_side(x, 0, 0, 0)
        one_device(d, lambda place: place < c * toks)

    def parts(chip, base):
        return (
            kvbuf[2 * chip, pl.ds(base, toks)],
            kvbuf[2 * chip + 1, pl.ds(base, toks)],
            kvbuf[2 * chip, pl.ds(base + toks, cached)],
            kvbuf[2 * chip + 1, pl.ds(base + toks, cached)],
        )

    def one_chip(t, g):
        j = z + (2 * g - 1) * t

        @pl.loop(0, NX)
        def _(o):
            @pl.when((o > 0) | (t > 0))
            def _():
                col = gk.column(o)
                gk.wait_side(col, o, t, g)
                chip = col * NZ + j
                seen = chip < x * NZ + z
                place = lax.broadcasted_iota(jnp.int32, (1, 2 * cached), 1) + chip * 2 * cached
                bias = jnp.where(place < begin, 0.0, LOW)

                @pl.when(seen)
                def _():
                    attend(
                        jnp.concatenate(parts(chip, 0), 0),
                        jnp.concatenate(parts(chip, half), 0),
                        jnp.concatenate([jnp.zeros((1, 2 * toks), F32), bias], 1),
                    )

                @pl.when(jnp.logical_not(seen))
                def _():
                    attend(
                        jnp.concatenate(parts(chip, 0)[2:], 0),
                        jnp.concatenate(parts(chip, half)[2:], 0),
                        bias,
                    )

    @pl.loop(0, NZ + 3)
    def _(t):
        @pl.when(t == 1)
        def _():
            sibling()

        @pl.loop(0, 2)
        def _(g):
            gk.stage_a(t, g)
            gk.stage_b(t - 1, g)
            gk.stage_c(t - 2, g)

            @pl.when(gk.ok(t - 3, g))
            def _():
                one_chip(t - 3, g)

    for head in range(GROUP):
        span = pl.ds(head * toks, toks)
        out_ref[:, pl.ds(head * HD, HD)] = (accum[span] / total[span]).astype(BF16)

    gw.finish_sends()
    gk.finish_sends()
    for slot in range(7):
        xcopy(tp, slot, over).wait_send()


def per_device(stream_x, norm_gain, w_qkv, cache_kv, recomp_hidden, recomp_index, prefix_len):
    toks, redo = stream_x.shape[0], recomp_hidden.shape[0]
    feats = stream_x.shape[1]
    cached = cache_kv.shape[1]
    seqs = NX * NZ * NC
    rows = toks + 16
    seq_at = lax.axis_index("seq")
    token_ids = seq_at * toks + jnp.arange(toks, dtype=jnp.int32)
    pad = jnp.zeros((rows - toks - redo,), jnp.int32)
    places = jnp.concatenate([token_ids + prefix_len[0], recomp_index, pad]).astype(F32)
    freq = jnp.exp(-math.log(1000000.0) * jnp.arange(HD // 2, dtype=F32) * 2.0 / HD)
    angle = places[:, None] * freq[None, :]
    cosine, sine = jnp.cos(angle), jnp.sin(angle)
    cosine = jnp.concatenate([cosine, cosine], 1)
    sine = jnp.concatenate([-sine, sine], 1)
    index = jnp.concatenate([recomp_index - seq_at * cached, pad - 1])[None, :]
    vmem = pl.BlockSpec(memory_space=pltpu.VMEM)
    return pl.pallas_call(
        kernel,
        out_shape=jax.ShapeDtypeStruct((toks, GROUP * HD), BF16),
        in_specs=[pl.BlockSpec(memory_space=pltpu.SMEM)] + [vmem] * 8,
        out_specs=vmem,
        scratch_shapes=[
            pltpu.VMEM((NY * NH, rows, feats), BF16),
            pltpu.VMEM((seqs,) + w_qkv.shape, BF16),
            pltpu.VMEM((seqs, 2 * (toks + cached), HD), BF16),
            pltpu.VMEM((rows, NY * NH * feats), BF16),
            pltpu.VMEM((rows, w_qkv.shape[1]), F32),
            pltpu.VMEM((GROUP * toks, HD), BF16),
            pltpu.VMEM((GROUP * toks, HD), F32),
            pltpu.VMEM((GROUP * toks, HD), F32),
            pltpu.VMEM((GROUP * toks, HD), F32),
            pltpu.SemaphoreType.DMA((7,)),
            pltpu.SemaphoreType.DMA((7,)),
            pltpu.SemaphoreType.DMA((4, NZ + 1, 2)),
            pltpu.SemaphoreType.DMA((4, NZ + 1, 2)),
            pltpu.SemaphoreType.DMA((4, NZ + 1, 2)),
            pltpu.SemaphoreType.DMA((4, NZ + 1, 2)),
            pltpu.SemaphoreType.DMA((6,)),
        ],
        compiler_params=pltpu.CompilerParams(
            collective_id=0, has_side_effects=True, vmem_limit_bytes=50 * 1024 * 1024
        ),
    )(
        prefix_len,
        stream_x,
        recomp_hidden,
        norm_gain[None, :],
        w_qkv,
        cache_kv,
        index,
        cosine,
        sine,
    )


def solution(mesh):
    placed = (
        P("seq", "tp"),
        P(),
        P("seq", "tp"),
        P(None, "seq", "tp"),
        P("seq", "tp"),
        P("seq"),
        P(),
    )
    return jax.shard_map(
        per_device, mesh=mesh, in_specs=placed, out_specs=P("seq", "tp"), check_vma=False
    )
```
